32 devices in a mesh: row: 8 (over z, y), col: 4 (over x, core).
Axes of the slice: x: 2, y: 2, z: 4, core: 2. Of those that a mesh axis runs over, the one named last changes fastest.
Arguments:
- eigvec: float32 [32, 8, 128, 1024], P(None, 'row', None, 'col'), may hold values from -6 to 6
- reflectors: float32 [2, 32, 8, 256, 128], P(None, None, 'row', 'col'), may hold values from -6 to 6
- sweep_group: int32 [2, 32, 8], P(None, None, 'row'), may hold values from -1 to 254, as said below
Outputs:
- transformed: float32 [32, 8, 128, 1024], P(None, 'row', None, 'col')
The draws below stay inside these ranges and needn't reach their ends.
Inputs may be any that keep to these rules, and one draw needn't show every extreme that they name: `sweep_group`: -1 where no diamond sits at that diagonal and tile position (tile position l * R + r for entry [d, l, r]); otherwise the diamond's sweep group, at most its tile position. Within one diagonal no two diamonds sit at adjacent tile positions, and none sits at the last tile position 255.
All inputs are finite; a program needn't handle non-finite values.
Results may differ from the reference program's by a relative error of at most 0.0003.
Values sent between devices are 32-bit elements.
No kernel may reach another device: no remote copies, remote signals or barrier semaphores. Data moves between devices by JAX's collectives and lax.ppermute only.
A program may use at most 128 MiB of HBM per device.

```python
import jax
import jax.numpy as jnp
from jax import lax

B = 128
DIAG = 2
NT = 256
TILES_DEV = 32
NC = 1024
N_ROW = 8


def draw_sweep_group(key, part):
    first_key = jax.random.fold_in(key, 11)
    second_key = jax.random.fold_in(key, 12)
    bits = jax.random.randint(first_key, (DIAG, NT), 0, 2).astype(jnp.int32)
    earlier = jnp.concatenate([jnp.zeros((DIAG, 1), jnp.int32), bits[:, :-1]], axis=1)
    positions = jnp.broadcast_to(jnp.arange(NT, dtype=jnp.int32)[None, :], (DIAG, NT))
    present = (bits == 1) & (earlier == 0) & (positions < NT - 1)
    groups = jax.random.randint(second_key, (DIAG, NT), 0, positions + 1).astype(jnp.int32)
    result = jnp.where(present, groups, -jnp.ones_like(groups))
    return result.reshape(DIAG, TILES_DEV, NT // TILES_DEV).astype(jnp.int32)


def level_of(key, dims, shards, least, largest):
    def one(dim, shards_of):
        steps = jax.random.uniform(jax.random.fold_in(jax.random.fold_in(key, 6), dim), (shards_of,), jnp.float32, least / len(shards), largest / len(shards))
        return jnp.repeat(jnp.exp(steps), dims[dim] // shards_of).reshape((-1,) + (1,) * (len(dims) - dim - 1))

    factor_of = one(*shards[0])
    for cut in shards[1:]:
        factor_of = factor_of * one(*cut)
    return factor_of


def gaussian(key, shape, deviation, reach, shards=(), kind=jnp.bfloat16):
    values = deviation * jax.random.normal(key, shape, jnp.float32)
    if shards:
        values = values * level_of(key, shape, shards, -0.22, 0.18)
    return jnp.clip(values, -reach, reach).astype(kind)


def setup_inputs(seed: int = 0) -> dict:
    streams_of = jax.random.split(jax.random.key(seed), 4)
    return {
        "eigvec": gaussian(streams_of[0], (TILES_DEV, N_ROW, B, NC), 1.0, 6.0, ((1, 8), (3, 4)), jnp.float32),
        "reflectors": gaussian(streams_of[1], (DIAG, TILES_DEV, N_ROW, 2 * B, B), 1.0, 6.0, ((2, 8), (3, 4)), jnp.float32),
        "sweep_group": draw_sweep_group(jax.random.fold_in(streams_of[3], 71), 0),
    }


highest_mode = lax.Precision.HIGHEST


def masked_vectors(panels):
    depth_rows = panels.shape[-2]
    band_width = panels.shape[-1]
    row_iota = lax.broadcasted_iota(jnp.int32, (depth_rows, band_width), 0)
    col_iota = lax.broadcasted_iota(jnp.int32, (depth_rows, band_width), 1)
    inside = (row_iota >= col_iota + 1) & (row_iota <= col_iota + band_width)
    leading = row_iota == col_iota + 1
    kept = jnp.where(inside, panels, jnp.zeros_like(panels))
    return jnp.where(leading, jnp.ones_like(panels), kept)


def inverse_factor(vectors):
    band_width = vectors.shape[-1]
    gram_matrix = jnp.einsum("...ji,...jk->...ik", vectors, vectors, precision=highest_mode)
    diagonal_part = jnp.diagonal(gram_matrix, axis1=-2, axis2=-1)
    strict_upper = jnp.triu(gram_matrix, 1)
    return strict_upper + jnp.eye(band_width, dtype=vectors.dtype) * (0.5 * diagonal_part[..., None, :])


def invert_upper(factor):
    band_width = factor.shape[-1]
    row_iota = lax.broadcasted_iota(jnp.int32, (band_width, band_width), 0)
    col_iota = lax.broadcasted_iota(jnp.int32, (band_width, band_width), 1)
    diagonal_part = jnp.diagonal(factor, axis1=-2, axis2=-1)
    eye_matrix = (row_iota == col_iota).astype(factor.dtype)
    inverse = eye_matrix * (1.0 / diagonal_part)[..., None, :]
    block = 1
    while block < band_width:
        coupling = ((row_iota // block) != (col_iota // block)) & ((row_iota // (2 * block)) == (col_iota // (2 * block)))
        upper_part = jnp.where(coupling, factor, jnp.zeros_like(factor))
        middle = jnp.einsum("...ij,...jk->...ik", upper_part, inverse, precision=highest_mode)
        inverse = inverse - jnp.einsum("...ij,...jk->...ik", inverse, middle, precision=highest_mode)
        block = block * 2
    return inverse


def reflect(stacked, vectors, factor):
    weights = jnp.einsum("...ji,...jc->...ic", vectors, stacked, precision=highest_mode)
    solved = jnp.einsum("...ik,...kc->...ic", invert_upper(factor), weights, precision=highest_mode)
    return stacked - jnp.einsum("...ji,...ic->...jc", vectors, solved, precision=highest_mode)


def apply_one(item):
    stacked, panels, flag = item
    vectors = masked_vectors(panels)
    factor = inverse_factor(vectors)
    updated = reflect(stacked, vectors, factor)
    return jnp.where(flag >= 0, updated, stacked)


def reference(eigvec, reflectors, sweep_group):
    tiles_dev = eigvec.shape[0]
    cycle_size = eigvec.shape[1]
    band = eigvec.shape[2]
    columns = eigvec.shape[3]
    total = tiles_dev * cycle_size
    diagonals = reflectors.shape[0]
    current = eigvec.reshape(total, band, columns)
    panels_all = reflectors.reshape(diagonals, total, 2 * band, band)
    flags_all = sweep_group.reshape(diagonals, total)
    for diagonal in range(diagonals):
        stacked = current.reshape(total // 2, 2 * band, columns)
        updated = lax.map(apply_one, (stacked, panels_all[diagonal, 0::2], flags_all[diagonal, 0::2]))
        current = updated.reshape(total, band, columns)
        inner = current[1:total - 1].reshape(total // 2 - 1, 2 * band, columns)
        updated = lax.map(apply_one, (inner, panels_all[diagonal, 1:total - 1:2], flags_all[diagonal, 1:total - 1:2]))
        current = jnp.concatenate([current[:1], updated.reshape(total - 2, band, columns), current[total - 1:]], axis=0)
    return current.reshape(tiles_dev, cycle_size, band, columns)
```

```python
import functools
import math

import jax
import jax.numpy as jnp
from jax import lax
from jax.experimental import pallas as pl
from jax.experimental.pallas import tpu as pltpu
from jax.sharding import PartitionSpec as P

f32, bf16, i32 = jnp.float32, jnp.bfloat16, jnp.int32
VMEM_LIMIT = 48 * 2**20


def split(x):
    high = x.astype(bf16)
    return high, (x - high.astype(f32)).astype(bf16)


def dot(a, b):
    return jnp.dot(a, b, preferred_element_type=f32)


def dot3(a, b):
    return dot(a[0], b[0]) + (dot(a[0], b[1]) + dot(a[1], b[0]))


def listed(active):
    tiles = active.shape[-1]
    place = lax.broadcasted_iota(i32, (tiles, tiles), 0)
    other = lax.broadcasted_iota(i32, (tiles, tiles), 1)
    numbers = active.astype(i32)
    rank = jnp.sum(jnp.where(other < place, numbers[:, None, :], 0), axis=-1)
    count = jnp.sum(numbers, axis=-1)
    wanted = jnp.minimum(place[None], count[:, None, None] - 1)
    chosen = active[:, None, :] & (rank[:, None, :] == wanted)
    return rank, count, chosen, jnp.sum(jnp.where(chosen, other, 0), axis=-1)


def tables(flags, row_index, row_count):
    active = flags >= 0
    own = lax.dynamic_index_in_dim(active, row_index, 0, keepdims=False)
    before = lax.dynamic_index_in_dim(
        active, lax.rem(row_index + row_count - 1, row_count), 0, keepdims=False
    )
    rank, count, chosen, own_list = listed(own)
    _, prior_count, _, prior_list = listed(before)
    shift = jnp.where(row_index == 0, 1, 0)
    prior_list = jnp.minimum(prior_list + shift, own.shape[-1] - 1)
    kept = jnp.where(own[0], rank[0] + 1, 0)
    slot = jnp.sum(jnp.where(chosen[1], kept[None, :], 0), axis=-1)
    counts = jnp.concatenate([count, prior_count])
    counts = jnp.pad(counts, (0, own.shape[-1] - 4))
    table = jnp.concatenate([own_list, prior_list, slot[None], counts[None]], axis=0)
    return table, jnp.max(jnp.sum(active.astype(i32), axis=-1))


OWN, PRIOR, SLOT, COUNTS = 0, 2, 4, 5


def take_body(row, cap, table, source, out, sems):
    copies = [
        pltpu.make_async_copy(source.at[table[row, k]], out.at[k], sems.at[k])
        for k in range(cap)
    ]
    for copy in copies:
        copy.start()
    for copy in copies:
        copy.wait()


def take(table, source, row, cap, name):
    shape = (cap,) + source.shape[1:]
    return pl.pallas_call(
        functools.partial(take_body, row, cap),
        out_shape=jax.ShapeDtypeStruct(shape, source.dtype),
        in_specs=[
            pl.BlockSpec(memory_space=pltpu.SMEM),
            pl.BlockSpec(memory_space=pl.ANY),
        ],
        out_specs=pl.BlockSpec(memory_space=pltpu.VMEM),
        scratch_shapes=[pltpu.SemaphoreType.DMA((cap,))],
        compiler_params=pltpu.CompilerParams(vmem_limit_bytes=16 * 2**20),
        cost_estimate=pl.CostEstimate(
            flops=10**7, bytes_accessed=8 * math.prod(shape), transcendentals=0
        ),
        name=name,
    )(table, source)


def put_body(diagonal, cap, table, tiles, current, out, sems):
    del current
    count = table[COUNTS, 2 + diagonal]
    copies = [
        pltpu.make_async_copy(
            tiles.at[k], out.at[table[PRIOR + diagonal, k]], sems.at[k]
        )
        for k in range(cap)
    ]
    for k, copy in enumerate(copies):
        pl.when(k < count)(copy.start)
    for k, copy in enumerate(copies):
        pl.when(k < count)(copy.wait)


def put(table, tiles, current, diagonal, name):
    cap = tiles.shape[0]
    return pl.pallas_call(
        functools.partial(put_body, diagonal, cap),
        out_shape=jax.ShapeDtypeStruct(current.shape, current.dtype),
        in_specs=[
            pl.BlockSpec(memory_space=pltpu.SMEM),
            pl.BlockSpec(memory_space=pltpu.VMEM),
            pl.BlockSpec(memory_space=pl.ANY),
        ],
        out_specs=pl.BlockSpec(memory_space=pl.ANY),
        input_output_aliases={2: 0},
        scratch_shapes=[pltpu.SemaphoreType.DMA((cap,))],
        compiler_params=pltpu.CompilerParams(vmem_limit_bytes=16 * 2**20),
        cost_estimate=pl.CostEstimate(
            flops=10**7, bytes_accessed=8 * tiles.size, transcendentals=0
        ),
        name=name,
    )(table, tiles, current)


def factor_body(diagonal, batch, table, packed, a_high, a_low, v_high, v_low):
    count = table[COUNTS, diagonal]

    @pl.when(pl.program_id(0) * batch < count)
    def _():
        band = packed.shape[-1]
        row = lax.broadcasted_iota(i32, (band, band), 0)
        col = lax.broadcasted_iota(i32, (band, band), 1)
        eye, upper = row == col, row < col
        transposed, couplings, inverses = [], [], []
        for b in range(batch):
            square = packed[b]
            first = jnp.where(row > col, square, 0.0)
            first = jnp.where(row == col + 1, 1.0, first)
            second = jnp.where(row > col, 0.0, square)
            second = jnp.where(col == row + band - 1, 1.0, second)
            vectors = jnp.concatenate([first, second], axis=0)
            halves = split(vectors)
            v_high[b], v_low[b] = halves
            turned = split(vectors.T)
            transposed.append(turned)
            gram = dot3(turned, halves)
            scale = jnp.where(eye, 2.0 / jnp.where(eye, gram, 1.0), 0.0)
            couplings.append(jnp.where(upper, gram, 0.0))
            pair = ((row >> 1) == (col >> 1)) & upper
            down = jnp.sum(scale, axis=1, keepdims=True)
            across = jnp.sum(scale, axis=0, keepdims=True)
            inverses.append(scale - jnp.where(pair, gram * down * across, 0.0))
        level = 1
        while 2**level < band:
            inside = ((row >> level) != (col >> level)) & (
                (row >> (level + 1)) == (col >> (level + 1))
            )
            pieces = [split(inverse) for inverse in inverses]
            middles = [
                dot3(split(jnp.where(inside, couplings[b], 0.0)), pieces[b])
                for b in range(batch)
            ]
            inverses = [
                inverses[b] - dot3(pieces[b], split(middles[b])) for b in range(batch)
            ]
            level += 1
        for b in range(batch):
            solver = dot3(split(inverses[b]), transposed[b])
            a_high[b], a_low[b] = split(solver)


def factors(table, packed, diagonal, name):
    cap, band = packed.shape[0], packed.shape[-1]
    batch = math.gcd(cap, 4)

    def at(i, table):
        return i, 0, 0

    wide = jax.ShapeDtypeStruct((cap, band, 2 * band), bf16)
    tall = jax.ShapeDtypeStruct((cap, 2 * band, band), bf16)
    return pl.pallas_call(
        functools.partial(factor_body, diagonal, batch),
        out_shape=(wide, wide, tall, tall),
        grid_spec=pltpu.PrefetchScalarGridSpec(
            num_scalar_prefetch=1,
            grid=(cap // batch,),
            in_specs=[pl.BlockSpec((batch, band, band), at)],
            out_specs=[
                pl.BlockSpec((batch, band, 2 * band), at),
                pl.BlockSpec((batch, band, 2 * band), at),
                pl.BlockSpec((batch, 2 * band, band), at),
                pl.BlockSpec((batch, 2 * band, band), at),
            ],
        ),
        compiler_params=pltpu.CompilerParams(vmem_limit_bytes=VMEM_LIMIT),
        cost_estimate=pl.CostEstimate(
            flops=cap * 60 * 6 * band**3, bytes_accessed=cap * 20 * band**2,
            transcendentals=0,
        ),
        name=name,
    )(table, packed)


def apply_body(diagonal, table, upper, beneath, kept, a_high, a_low, v_high, v_low, new_upper, lower):
    step = pl.program_id(0)
    count = table[COUNTS, diagonal]

    @pl.when(step < count)
    def _():
        band = upper.shape[1]
        top = upper[0]
        low = beneath[0]
        if diagonal:
            low = jnp.where(table[SLOT, step] > 0, kept[0], low)
        stacked = jnp.concatenate([top, low], axis=0)
        solved = dot3((a_high[0], a_low[0]), split(stacked))
        updated = stacked - dot3((v_high[0], v_low[0]), split(solved))
        new_upper[0] = updated[:band]
        lower[0] = updated[band:]

    @pl.when((count == 0) & (step == 0))
    def _():
        new_upper[...] = upper[...]


def apply(table, current, beneath, kept, parts, diagonal, name):
    cap, band, columns = beneath.shape

    def slot_of(i, table):
        return jnp.maximum(jnp.minimum(i, table[COUNTS, diagonal] - 1), 0)

    def own(i, table):
        return table[OWN + diagonal, i], 0, 0

    def compact(i, table):
        return slot_of(i, table), 0, 0

    def earlier(i, table):
        if not diagonal:
            return 0, 0, 0
        return jnp.maximum(table[SLOT, i] - 1, 0), 0, 0

    tile = (1, band, columns)
    return pl.pallas_call(
        functools.partial(apply_body, diagonal),
        out_shape=(
            jax.ShapeDtypeStruct(current.shape, f32),
            jax.ShapeDtypeStruct(beneath.shape, f32),
        ),
        grid_spec=pltpu.PrefetchScalarGridSpec(
            num_scalar_prefetch=1,
            grid=(cap,),
            in_specs=[
                pl.BlockSpec(tile, own),
                pl.BlockSpec(tile, compact),
                pl.BlockSpec(tile, earlier),
                pl.BlockSpec((1, band, 2 * band), compact),
                pl.BlockSpec((1, band, 2 * band), compact),
                pl.BlockSpec((1, 2 * band, band), compact),
                pl.BlockSpec((1, 2 * band, band), compact),
            ],
            out_specs=[pl.BlockSpec(tile, own), pl.BlockSpec(tile, compact)],
        ),
        input_output_aliases={1: 0},
        compiler_params=pltpu.CompilerParams(vmem_limit_bytes=VMEM_LIMIT),
        cost_estimate=pl.CostEstimate(
            flops=cap * 24 * band * band * columns, bytes_accessed=cap * 28 * band * columns,
            transcendentals=0,
        ),
        name=name,
    )(table, current, beneath, kept, *parts)


def whole_panels(shards):
    columns = lax.axis_size("col")
    half = columns // 2
    here = lax.axis_index("col")
    rows, band = shards.shape[-2:]
    across = lax.ppermute(
        shards, "col", [(i, (i + half) % columns) for i in range(columns)]
    )
    group = lax.rem(here, half)
    row = lax.broadcasted_iota(i32, (rows, band), 0) + group * rows
    col = lax.broadcasted_iota(i32, (rows, band), 1)
    mine = jnp.where(
        ((row > col) == (here < half))[None], shards, across
    )
    pieces = [mine]
    for by in range(1, half):
        pieces.append(
            lax.ppermute(
                mine, "col",
                [(i, i // half * half + (i + by) % half) for i in range(columns)],
            )
        )
    ordered = [
        lax.select_n(lax.rem(group - place + half, half), *pieces) if half > 1 else mine
        for place in range(half)
    ] if half != 2 else [
        jnp.where(group == place, pieces[0], pieces[1]) for place in range(half)
    ]
    return jnp.concatenate(ordered, axis=-2)


def up(tiles):
    count = lax.axis_size("row")
    return lax.ppermute(tiles, "row", [(i, (i - 1) % count) for i in range(count)])


def down(tiles):
    count = lax.axis_size("row")
    return lax.ppermute(tiles, "row", [(i, (i + 1) % count) for i in range(count)])


def with_capacity(cap, eigvec, reflectors, table):
    shards = [take(table, reflectors[d], OWN + d, cap, f"panels{d}") for d in range(2)]
    leaving = take(table, eigvec, PRIOR, cap, "leave0")
    beneath = up(leaving)
    parts = [factors(table, whole_panels(shards[d]), d, f"factors{d}") for d in range(2)]
    current, lower = apply(table, eigvec, beneath, beneath, parts[0], 0, "apply0")
    leaving = take(table, current, PRIOR + 1, cap, "leave1")
    returned = down(lower)
    beneath = up(leaving)
    current = put(table, returned, current, 0, "arrive0")
    current, lower = apply(table, current, beneath, lower, parts[1], 1, "apply1")
    returned = down(lower)
    return put(table, returned, current, 1, "arrive1")


def local(eigvec, reflectors, sweep_group):
    tiles = eigvec.shape[0]
    flags = lax.all_gather(sweep_group[:, :, 0], "row")
    table, most = tables(flags, lax.axis_index("row"), lax.axis_size("row"))
    caps = (tiles * 3 // 8, tiles // 2, tiles)
    which = (most > caps[0]).astype(i32) + (most > caps[1]).astype(i32)
    branches = [functools.partial(with_capacity, cap) for cap in caps]
    out = lax.switch(which, branches, eigvec[:, 0], reflectors[:, :, 0], table)
    return out[:, None]


def solution(mesh):
    return jax.shard_map(
        local,
        mesh=mesh,
        in_specs=(
            P(None, "row", None, "col"),
            P(None, None, "row", "col", None),
            P(None, None, "row"),
        ),
        out_specs=P(None, "row", None, "col"),
        check_vma=False,
    )
```

```python
import functools
import math

import jax
import jax.numpy as jnp
from jax import lax
from jax.experimental import pallas as pl
from jax.experimental.pallas import tpu as pltpu
from jax.sharding import PartitionSpec as P

f32, bf16, i32 = jnp.float32, jnp.bfloat16, jnp.int32
VMEM_LIMIT = 48 * 2**20


def split(x):
    high = x.astype(bf16)
    return high, (x - high.astype(f32)).astype(bf16)


def dot(a, b):
    return jnp.dot(a, b, preferred_element_type=f32)


def dot3(a, b):
    return dot(a[0], b[0]) + (dot(a[0], b[1]) + dot(a[1], b[0]))


def listed(active):
    tiles = active.shape[-1]
    place = lax.broadcasted_iota(i32, (tiles, tiles), 0)
    other = lax.broadcasted_iota(i32, (tiles, tiles), 1)
    numbers = active.astype(i32)
    rank = jnp.sum(jnp.where(other < place, numbers[:, None, :], 0), axis=-1)
    count = jnp.sum(numbers, axis=-1)
    wanted = jnp.minimum(place[None], count[:, None, None] - 1)
    chosen = active[:, None, :] & (rank[:, None, :] == wanted)
    return rank, count, chosen, jnp.sum(jnp.where(chosen, other, 0), axis=-1)


def own_table(own):
    rank, count, chosen, own_list = listed(own)
    kept = jnp.where(own[0], rank[0] + 1, 0)
    slot = jnp.sum(jnp.where(chosen[1], kept[None, :], 0), axis=-1)
    counts = jnp.pad(count, (0, own.shape[-1] - 2))
    return jnp.concatenate(
        [own_list, jnp.zeros_like(own_list), slot[None], counts[None]], axis=0
    )


def whole_table(table, flags, row_index, row_count):
    active = flags >= 0
    before = lax.dynamic_index_in_dim(
        active, lax.rem(row_index + row_count - 1, row_count), 0, keepdims=False
    )
    _, count, _, prior_list = listed(before)
    tiles = before.shape[-1]
    shift = jnp.where(row_index == 0, 1, 0)
    prior_list = jnp.minimum(prior_list + shift, tiles - 1)
    zero = jnp.zeros((1, tiles), i32)
    counts = jnp.pad(count, (2, tiles - 4))
    table = table + jnp.concatenate(
        [zero, zero, prior_list, zero, counts[None]], axis=0
    )
    return table, jnp.max(jnp.sum(active.astype(i32), axis=-1))


OWN, PRIOR, SLOT, COUNTS = 0, 2, 4, 5


def take_body(row, cap, table, source, out, sems):
    copies = [
        pltpu.make_async_copy(source.at[table[row, k]], out.at[k], sems.at[k])
        for k in range(cap)
    ]
    for copy in copies:
        copy.start()
    for copy in copies:
        copy.wait()


def take(table, source, row, cap, name):
    shape = (cap,) + source.shape[1:]
    return pl.pallas_call(
        functools.partial(take_body, row, cap),
        out_shape=jax.ShapeDtypeStruct(shape, source.dtype),
        in_specs=[
            pl.BlockSpec(memory_space=pltpu.SMEM),
            pl.BlockSpec(memory_space=pl.ANY),
        ],
        out_specs=pl.BlockSpec(memory_space=pltpu.VMEM),
        scratch_shapes=[pltpu.SemaphoreType.DMA((cap,))],
        compiler_params=pltpu.CompilerParams(vmem_limit_bytes=16 * 2**20),
        cost_estimate=pl.CostEstimate(
            flops=10**7, bytes_accessed=8 * math.prod(shape), transcendentals=0
        ),
        name=name,
    )(table, source)


def put_body(diagonal, cap, table, tiles, current, out, sems):
    del current
    count = table[COUNTS, 2 + diagonal]
    copies = [
        pltpu.make_async_copy(
            tiles.at[k], out.at[table[PRIOR + diagonal, k]], sems.at[k]
        )
        for k in range(cap)
    ]
    for k, copy in enumerate(copies):
        pl.when(k < count)(copy.start)
    for k, copy in enumerate(copies):
        pl.when(k < count)(copy.wait)


def put(table, tiles, current, diagonal, name):
    cap = tiles.shape[0]
    return pl.pallas_call(
        functools.partial(put_body, diagonal, cap),
        out_shape=jax.ShapeDtypeStruct(current.shape, current.dtype),
        in_specs=[
            pl.BlockSpec(memory_space=pltpu.SMEM),
            pl.BlockSpec(memory_space=pltpu.VMEM),
            pl.BlockSpec(memory_space=pl.ANY),
        ],
        out_specs=pl.BlockSpec(memory_space=pl.ANY),
        input_output_aliases={2: 0},
        scratch_shapes=[pltpu.SemaphoreType.DMA((cap,))],
        compiler_params=pltpu.CompilerParams(vmem_limit_bytes=16 * 2**20),
        cost_estimate=pl.CostEstimate(
            flops=10**7, bytes_accessed=8 * tiles.size, transcendentals=0
        ),
        name=name,
    )(table, tiles, current)


def factor_body(diagonal, batch, table, packed, a_high, a_low, v_high, v_low):
    count = table[COUNTS, diagonal]

    @pl.when(pl.program_id(0) * batch < count)
    def _():
        band = packed.shape[-1]
        row = lax.broadcasted_iota(i32, (band, band), 0)
        col = lax.broadcasted_iota(i32, (band, band), 1)
        eye, upper = row == col, row < col
        transposed, couplings, inverses = [], [], []
        for b in range(batch):
            square = packed[b]
            first = jnp.where(row > col, square, 0.0)
            first = jnp.where(row == col + 1, 1.0, first)
            second = jnp.where(row > col, 0.0, square)
            second = jnp.where(col == row + band - 1, 1.0, second)
            vectors = jnp.concatenate([first, second], axis=0)
            halves = split(vectors)
            v_high[b], v_low[b] = halves
            turned = split(vectors.T)
            transposed.append(turned)
            gram = dot3(turned, halves)
            scale = jnp.where(eye, 2.0 / jnp.where(eye, gram, 1.0), 0.0)
            couplings.append(jnp.where(upper, gram, 0.0))
            pair = ((row >> 1) == (col >> 1)) & upper
            down = jnp.sum(scale, axis=1, keepdims=True)
            across = jnp.sum(scale, axis=0, keepdims=True)
            inverses.append(scale - jnp.where(pair, gram * down * across, 0.0))
        level = 1
        while 2**level < band:
            inside = ((row >> level) != (col >> level)) & (
                (row >> (level + 1)) == (col >> (level + 1))
            )
            pieces = [split(inverse) for inverse in inverses]
            middles = [
                dot3(split(jnp.where(inside, couplings[b], 0.0)), pieces[b])
                for b in range(batch)
            ]
            inverses = [
                inverses[b] - dot3(pieces[b], split(middles[b])) for b in range(batch)
            ]
            level += 1
        for b in range(batch):
            solver = dot3(split(inverses[b]), transposed[b])
            a_high[b], a_low[b] = split(solver)


def factors(table, packed, diagonal, name):
    cap, band = packed.shape[0], packed.shape[-1]
    batch = math.gcd(cap, 2)

    def at(i, table):
        return i, 0, 0

    wide = jax.ShapeDtypeStruct((cap, band, 2 * band), bf16)
    tall = jax.ShapeDtypeStruct((cap, 2 * band, band), bf16)
    return pl.pallas_call(
        functools.partial(factor_body, diagonal, batch),
        out_shape=(wide, wide, tall, tall),
        grid_spec=pltpu.PrefetchScalarGridSpec(
            num_scalar_prefetch=1,
            grid=(cap // batch,),
            in_specs=[pl.BlockSpec((batch, band, band), at)],
            out_specs=[
                pl.BlockSpec((batch, band, 2 * band), at),
                pl.BlockSpec((batch, band, 2 * band), at),
                pl.BlockSpec((batch, 2 * band, band), at),
                pl.BlockSpec((batch, 2 * band, band), at),
            ],
        ),
        compiler_params=pltpu.CompilerParams(vmem_limit_bytes=VMEM_LIMIT),
        cost_estimate=pl.CostEstimate(
            flops=cap * 60 * 6 * band**3, bytes_accessed=cap * 20 * band**2,
            transcendentals=0,
        ),
        name=name,
    )(table, packed)


def apply_body(diagonal, table, upper, beneath, kept, a_high, a_low, v_high, v_low, new_upper, lower):
    step = pl.program_id(0)
    count = table[COUNTS, diagonal]

    @pl.when(step < count)
    def _():
        band = upper.shape[1]
        top = upper[0]
        low = beneath[0]
        if diagonal:
            low = jnp.where(table[SLOT, step] > 0, kept[0], low)
        stacked = jnp.concatenate([top, low], axis=0)
        solved = dot3((a_high[0], a_low[0]), split(stacked))
        updated = stacked - dot3((v_high[0], v_low[0]), split(solved))
        new_upper[0] = updated[:band]
        lower[0] = updated[band:]

    @pl.when((count == 0) & (step == 0))
    def _():
        new_upper[...] = upper[...]


def apply(table, current, beneath, kept, parts, diagonal, name):
    cap, band, columns = beneath.shape

    def slot_of(i, table):
        return jnp.maximum(jnp.minimum(i, table[COUNTS, diagonal] - 1), 0)

    def own(i, table):
        return table[OWN + diagonal, i], 0, 0

    def compact(i, table):
        return slot_of(i, table), 0, 0

    def earlier(i, table):
        if not diagonal:
            return 0, 0, 0
        return jnp.maximum(table[SLOT, i] - 1, 0), 0, 0

    tile = (1, band, columns)
    return pl.pallas_call(
        functools.partial(apply_body, diagonal),
        out_shape=(
            jax.ShapeDtypeStruct(current.shape, f32),
            jax.ShapeDtypeStruct(beneath.shape, f32),
        ),
        grid_spec=pltpu.PrefetchScalarGridSpec(
            num_scalar_prefetch=1,
            grid=(cap,),
            in_specs=[
                pl.BlockSpec(tile, own),
                pl.BlockSpec(tile, compact),
                pl.BlockSpec(tile, earlier),
                pl.BlockSpec((1, band, 2 * band), compact),
                pl.BlockSpec((1, band, 2 * band), compact),
                pl.BlockSpec((1, 2 * band, band), compact),
                pl.BlockSpec((1, 2 * band, band), compact),
            ],
            out_specs=[pl.BlockSpec(tile, own), pl.BlockSpec(tile, compact)],
        ),
        input_output_aliases={1: 0},
        compiler_params=pltpu.CompilerParams(vmem_limit_bytes=VMEM_LIMIT),
        cost_estimate=pl.CostEstimate(
            flops=cap * 24 * band * band * columns, bytes_accessed=cap * 28 * band * columns,
            transcendentals=0,
        ),
        name=name,
    )(table, current, beneath, kept, *parts)


def own_rows(shards):
    columns = lax.axis_size("col")
    half = columns // 2
    here = lax.axis_index("col")
    rows, band = shards.shape[-2:]
    across = lax.ppermute(
        shards, "col", [(i, (i + half) % columns) for i in range(columns)]
    )
    row = lax.broadcasted_iota(i32, (rows, band), 0) + lax.rem(here, half) * rows
    col = lax.broadcasted_iota(i32, (rows, band), 1)
    return jnp.where(((row > col) == (here < half))[None], shards, across)


def squares(mine):
    columns = lax.axis_size("col")
    half = columns // 2
    group = lax.rem(lax.axis_index("col"), half)
    pieces = [mine]
    for by in range(1, half):
        pairs = [(i, i // half * half + (i + by) % half) for i in range(columns)]
        pieces.append(lax.ppermute(mine, "col", pairs))
    ordered = []
    for place in range(half):
        wanted = lax.rem(group - place + half, half)
        chosen = pieces[0]
        for by in range(1, half):
            chosen = jnp.where(wanted == by, pieces[by], chosen)
        ordered.append(chosen)
    return jnp.concatenate(ordered, axis=-2)


def up(tiles):
    count = lax.axis_size("row")
    return lax.ppermute(tiles, "row", [(i, (i - 1) % count) for i in range(count)])


def down(tiles):
    count = lax.axis_size("row")
    return lax.ppermute(tiles, "row", [(i, (i + 1) % count) for i in range(count)])


def panels_of(table, reflectors, cap):
    return [take(table, reflectors[d], OWN + d, cap, f"panels{d}") for d in range(2)]


def with_capacity(cap, everything, eigvec, reflectors, table, mine):
    leaving = take(table, eigvec, PRIOR, cap, "leave0")
    if everything:
        mine = [own_rows(shard) for shard in panels_of(table, reflectors, cap)]
    leaving, mine = lax.optimization_barrier((leaving, mine))
    beneath = up(leaving)
    parts = [factors(table, squares(mine[d]), d, f"factors{d}") for d in range(2)]
    current, lower = apply(table, eigvec, beneath, beneath, parts[0], 0, "apply0")
    leaving = take(table, current, PRIOR + 1, cap, "leave1")
    returned = down(lower)
    beneath = up(leaving)
    current = put(table, returned, current, 0, "arrive0")
    current, lower = apply(table, current, beneath, lower, parts[1], 1, "apply1")
    returned = down(lower)
    return put(table, returned, current, 1, "arrive1")


def local(eigvec, reflectors, sweep_group):
    tiles = eigvec.shape[0]
    groups = sweep_group[:, :, 0]
    reflectors = reflectors[:, :, 0]
    half = max(tiles // 2, 1)
    table = own_table(groups >= 0)
    shards, groups = lax.optimization_barrier(
        (panels_of(table, reflectors, half), groups)
    )
    flags = lax.all_gather(groups, "row")
    mine = [own_rows(shard) for shard in shards]
    table, most = whole_table(
        table, flags, lax.axis_index("row"), lax.axis_size("row")
    )
    sizes = {max(tiles * k // 32, 1) for k in (12, 13, 14)}
    caps = sorted(sizes | {half, tiles})
    which = sum((most > cap).astype(i32) for cap in caps[:-1])
    branches = [functools.partial(with_capacity, cap, cap > half) for cap in caps]
    out = lax.switch(which, branches, eigvec[:, 0], reflectors, table, mine)
    return out[:, None]


def solution(mesh):
    return jax.shard_map(
        local,
        mesh=mesh,
        in_specs=(
            P(None, "row", None, "col"),
            P(None, None, "row", "col", None),
            P(None, None, "row"),
        ),
        out_specs=P(None, "row", None, "col"),
        check_vma=False,
    )
```
